32 devices in a mesh: row: 8 (over z, core), aux: 4 (over y, x).
Axes of the slice: x: 2, y: 2, z: 4, core: 2. Of those that a mesh axis runs over, the one named last changes fastest.
Arguments:
- factor_ia: float32 [64, 12288], P('row', 'aux'), may hold values from -0.8 to 0.8
- factor_jb: float32 [5120, 12288], P('row', 'aux'), may hold values from -0.8 to 0.8
- denominators: float32 [64, 5120], P(None, 'row'), may hold values from 0.5 to 8
Outputs:
- grad_jb: float32 [5120, 12288], P('row', 'aux')
- grad_ia: float32 [64, 12288], P('row', 'aux')
The draws below stay inside these ranges and needn't reach their ends.
All inputs are finite; a program needn't handle non-finite values.
Results may differ from the reference program's by a relative error of at most 0.00011.
Values sent between devices are 32-bit elements; how exact they have to be, the bound alone decides.
No kernel may reach another device: no remote copies, remote signals or barrier semaphores. Data moves between devices by JAX's collectives and lax.ppermute only.
A program may use at most 64 MiB of HBM per device.

```python
import math
import jax
import jax.numpy as jnp
from jax import lax

NAUX = 12288
JB = 5120
IA = 64


def steps_of(own_key, dims, pieces, least, largest):
    gain = 1.0
    for axis_at, blocks in pieces:
        heights = jax.random.uniform(jax.random.fold_in(jax.random.fold_in(own_key, 6), axis_at), (blocks,), jnp.float32, least / len(pieces), largest / len(pieces))
        gain = gain * jnp.repeat(jnp.exp(heights), dims[axis_at] // blocks).reshape((-1,) + (1,) * (len(dims) - 1 - axis_at))
    return gain


def bell_draw(stream_key, shape, spread, limit, cuts=(), dtype=jnp.bfloat16):
    level = steps_of(stream_key, shape, cuts, -0.22, 0.18) if cuts else 1.0
    array = jax.random.normal(stream_key, shape, jnp.float32) * spread * level
    return jnp.minimum(jnp.maximum(array, -limit), limit).astype(dtype)


def setup_inputs(seed: int = 0) -> dict:
    arg_keys = jax.random.split(jax.random.key(seed), 4)
    return {
        "factor_ia": bell_draw(arg_keys[0], (IA, NAUX), 0.1, 0.8, ((0, 8), (1, 4)), jnp.float32),
        "factor_jb": bell_draw(arg_keys[1], (JB, NAUX), 0.1, 0.8, ((0, 8), (1, 4)), jnp.float32),
        "denominators": jnp.clip(jnp.exp(math.log(8.0) - 2.7725887 * jax.random.uniform(arg_keys[2], (IA, JB), jnp.float32) ** steps_of(arg_keys[2], (IA, JB), ((1, 8),), -0.2, 0.2)), 0.5, 8.0),
    }


def reference(factor_ia, factor_jb, denominators):
    integrals = lax.dot_general(factor_ia, factor_jb, (((1,), (1,)), ((), ())), precision=lax.Precision.HIGHEST, preferred_element_type=jnp.float32)
    amplitudes = integrals / denominators
    grad_jb = lax.dot_general(amplitudes, factor_ia, (((0,), (0,)), ((), ())), precision=lax.Precision.HIGHEST, preferred_element_type=jnp.float32)
    grad_ia = jnp.dot(amplitudes, factor_jb, precision=lax.Precision.HIGHEST, preferred_element_type=jnp.float32)
    return grad_jb, grad_ia
```

```python
import jax
import jax.numpy as jnp
from jax import lax
from jax.sharding import PartitionSpec as P

HIGH = lax.Precision.HIGH


def swap(x, axis, distance):
    size = lax.axis_size(axis)
    return lax.ppermute(x, axis, [(i, i ^ distance) for i in range(size)])


def dot(a, b, dims):
    return lax.dot_general(a, b, (dims, ((), ())), precision=HIGH, preferred_element_type=jnp.float32)


def per_device(factor_ia, factor_jb, denominators):
    rows = lax.axis_size("row")
    aux = lax.axis_size("aux")
    me = lax.axis_index("row")
    height = factor_ia.shape[0]

    far = [swap(factor_ia, "row", d) for d in range(rows - 2, 0, -2)][::-1]
    even = jnp.stack([factor_ia] + far)
    odd = swap(even, "row", 1)
    whole_ia = jnp.stack([even, odd], axis=1).reshape(rows * height, -1)
    denom = jnp.concatenate(
        [lax.dynamic_slice_in_dim(denominators, (me ^ d) * height, height, 0) for d in range(rows)]
    )

    integrals = dot(whole_ia, factor_jb, ((1,), (1,)))
    step = 1
    while step < aux:
        integrals = integrals + swap(integrals, "aux", step)
        step *= 2
    amplitudes = integrals / denom

    partial = dot(amplitudes, factor_jb, ((1,), (0,))).reshape(rows // 2, 2, height, -1)
    summed = partial[:, 0] + swap(partial[:, 1], "row", 1)
    grad_ia = summed[0]
    for part in [swap(summed[d // 2], "row", d) for d in range(rows - 2, 0, -2)]:
        grad_ia = grad_ia + part
    grad_jb = dot(amplitudes, whole_ia, ((0,), (0,)))
    return (grad_jb, grad_ia)


def solution(mesh):
    return jax.shard_map(
        per_device,
        mesh=mesh,
        in_specs=(P("row", "aux"), P("row", "aux"), P(None, "row")),
        out_specs=(P("row", "aux"), P("row", "aux")),
        check_vma=False,
    )
```

```python
import jax
import jax.numpy as jnp
from jax import lax
from jax.experimental import pallas as pl
from jax.experimental.pallas import tpu as pltpu
from jax.sharding import PartitionSpec as P


F32, BF16 = jnp.float32, jnp.bfloat16
VMEM = pl.BlockSpec(memory_space=pltpu.VMEM)
HBM = pl.BlockSpec(memory_space=pltpu.HBM)
MIB = 1 << 20
TILE = 128
FIRST = 3


def swap(x, axis, distance):
    size = lax.axis_size(axis)
    return lax.ppermute(x, axis, [(i, i ^ distance) for i in range(size)])


def split(x):
    hi = x.astype(BF16)
    return hi, (x - hi.astype(F32)).astype(BF16)


def mxu(a, b, dims):
    return lax.dot_general(a, b, (dims, ((), ())), preferred_element_type=F32)


def width_of(size, most):
    fits = [w for w in range(128, min(size, most) + 1, 128) if size % w == 0]
    return fits[-1] if fits else size


def prepare(factor_jb):
    height, width = factor_jb.shape
    pieces = [p for p in (8, 4, 2, 1) if height % (16 * p) == 0][0]
    piece = height // pieces

    def kernel(jb, hi, lo, held, sems):
        def copy(p):
            at = pl.ds(p * piece, piece)
            return pltpu.make_async_copy(jb.at[at], held.at[at], sems.at[p])

        for p in range(pieces):
            copy(p).start()
        for p in range(pieces):
            copy(p).wait()

            @pl.loop(0, piece, step=16)
            def _(r, p=p):
                at = pl.ds(p * piece + r, 16)
                hi[at], lo[at] = split(held[at])

    out = jax.ShapeDtypeStruct((height, width), BF16)
    return pl.pallas_call(
        kernel,
        name="prepare",
        out_shape=(out, out),
        in_specs=[HBM],
        out_specs=(VMEM, VMEM),
        scratch_shapes=[pltpu.VMEM((height, width), F32), pltpu.SemaphoreType.DMA((pieces,))],
        compiler_params=pltpu.CompilerParams(vmem_limit_bytes=44 * MIB),
        cost_estimate=pl.CostEstimate(flops=4 * height * width, bytes_accessed=4 * height * width, transcendentals=0),
    )(factor_jb)


def integral_share(blocks, jb_hi, jb_lo, columns, parts=None):
    n = len(blocks)
    height, width = blocks[0].shape
    rows = n * height
    start, count = columns

    def kernel(*refs):
        block_refs, (hi, lo, out, parts) = refs[:n], refs[n : n + 4]
        for pair in range(n // 2):
            x = jnp.concatenate([block_refs[2 * pair][...], block_refs[2 * pair + 1][...]])
            a, b = split(x)
            at = 2 * height * pair
            parts[pl.ds(at, 2 * height)] = a
            parts[pl.ds(rows + at, 2 * height)] = b
        multiply(parts, hi, lo, out)

    def again(parts, hi, lo, out):
        multiply(parts, hi, lo, out)

    def multiply(parts, hi, lo, out):
        for t in range(0, count, TILE):
            at = pl.ds(start + t, TILE)
            both = mxu(parts[...], hi[at], ((1,), (1,)))
            rest = mxu(parts[pl.ds(0, rows)], lo[at], ((1,), (1,)))
            out[:, pl.ds(t, TILE)] = both[:rows] + (both[rows:] + rest)

    out = jax.ShapeDtypeStruct((rows, count), F32)
    stacked = jax.ShapeDtypeStruct((2 * rows, width), BF16)
    first = parts is None
    return pl.pallas_call(
        kernel if first else again,
        out_shape=(out, stacked) if first else out,
        in_specs=[VMEM] * (n + 2 if first else 3),
        out_specs=(VMEM, VMEM) if first else VMEM,
        compiler_params=pltpu.CompilerParams(vmem_limit_bytes=30 * MIB),
        cost_estimate=pl.CostEstimate(flops=6 * rows * width * count, bytes_accessed=MIB, transcendentals=0),
    )(*(blocks if first else [parts]), jb_hi, jb_lo)


def gradient_share(mine, theirs, denominators, jb_hi, jb_lo, distances, columns, height, before=None):
    rows = mine.shape[0]
    width = jb_hi.shape[1]
    n = len(distances)
    tile = width_of(width, 512)
    start, count = columns
    last = before is not None

    def kernel(*refs):
        mine, theirs, denom, hi, lo = refs[:5]
        parts, *outs, amp = refs[5 + last :]
        me = lax.axis_index("row")
        for slot, d in enumerate(distances):
            at = pl.multiple_of((me ^ d) * height, height)
            here = pl.ds(slot * height, height)
            amp[here] = (mine[here] + theirs[here]) / denom[pl.ds(at, height), pl.ds(start, count)]
        a, b = split(amp[...])
        parts[pl.ds(0, rows)] = a
        parts[pl.ds(rows, rows)] = b
        for t in range(width // tile):
            at = pl.ds(t * tile, tile)
            both = mxu(parts[...], hi[pl.ds(start, count), at], ((1,), (0,)))
            rest = mxu(parts[pl.ds(0, rows)], lo[pl.ds(start, count), at], ((1,), (0,)))
            total = both[:rows] + (both[rows:] + rest)
            if last:
                total = refs[5][:, at] + total
                for slot in range(n):
                    outs[slot % 2][slot // 2, :, at] = total[slot * height : (slot + 1) * height]
            else:
                outs[0][:, at] = total

    half = jax.ShapeDtypeStruct((n // 2, height, width), F32)
    outs = (half, half) if last else (jax.ShapeDtypeStruct((rows, width), F32),)
    args = (mine, theirs, denominators, jb_hi, jb_lo) + ((before,) if last else ())
    return pl.pallas_call(
        kernel,
        out_shape=(jax.ShapeDtypeStruct((2 * rows, count), BF16), *outs),
        in_specs=[VMEM] * len(args),
        out_specs=(VMEM,) * (1 + len(outs)),
        scratch_shapes=[pltpu.VMEM((rows, count), F32)],
        compiler_params=pltpu.CompilerParams(vmem_limit_bytes=30 * MIB),
        cost_estimate=pl.CostEstimate(flops=6 * rows * width * count, bytes_accessed=MIB, transcendentals=0),
    )(*args)


def gradient_jb(amp_parts, ia_parts):
    rows, width = ia_parts.shape[0] // 2, ia_parts.shape[1]
    first, second = (a.shape[1] // TILE for a in amp_parts)

    def kernel(one, two, ia, out):
        amp = jnp.where(pl.program_id(0) < first, one[...].astype(F32), two[...].astype(F32))
        a_hi, a_lo = amp[:rows], amp[rows:]
        i_hi, i_lo = ia[pl.ds(0, rows)], ia[pl.ds(rows, rows)]
        left = jnp.concatenate([a_hi, a_lo, a_hi]).T.astype(BF16)
        out[...] = mxu(left, jnp.concatenate([i_hi, i_hi, i_lo]), ((1,), (0,)))

    return pl.pallas_call(
        kernel,
        name="gradient_jb",
        grid=(first + second,),
        out_shape=jax.ShapeDtypeStruct(((first + second) * TILE, width), F32),
        in_specs=[
            pl.BlockSpec((2 * rows, TILE), lambda t: (0, jnp.minimum(t, first - 1))),
            pl.BlockSpec((2 * rows, TILE), lambda t: (0, jnp.maximum(t - first, 0))),
            pl.BlockSpec((2 * rows, width), lambda t: (0, 0)),
        ],
        out_specs=pl.BlockSpec((TILE, width), lambda t: (t, 0)),
        compiler_params=pltpu.CompilerParams(vmem_limit_bytes=30 * MIB),
        cost_estimate=pl.CostEstimate(
            flops=6 * rows * width * (first + second) * TILE,
            bytes_accessed=4 * width * (first + second) * TILE,
            transcendentals=0,
        ),
    )(*amp_parts, ia_parts)


def chip_order(rows):
    chips = rows // 2
    return [k for k in (2, 1, *range(3, chips)) if k < chips]


def aux_order(aux, chunk):
    steps = [1 << b for b in range(aux.bit_length() - 1)]
    return steps[::-1] if chunk else steps


def per_device(factor_ia, factor_jb, denominators):
    rows = lax.axis_size("row")
    aux = lax.axis_size("aux")
    height = factor_ia.shape[0]
    tiles = factor_jb.shape[0] // TILE
    cut = FIRST * tiles // 5 * TILE
    chunks = [(0, cut), (cut, tiles * TILE - cut)]

    blocks = {0: factor_ia}
    for k in chip_order(rows):
        blocks[2 * k] = swap(factor_ia, "row", 2 * k)
    for d in range(0, rows, 2):
        blocks[d + 1] = swap(blocks[d], "row", 1)
    jb_hi, jb_lo = prepare(factor_jb)

    ordered = [blocks[d] for d in range(rows)]
    share0, ia_parts = integral_share(ordered, jb_hi, jb_lo, chunks[0])
    share1 = integral_share(ordered, jb_hi, jb_lo, chunks[1], ia_parts)
    amp_parts, outs = [], [None]
    for c, share in enumerate((share0, share1)):
        *steps, step = aux_order(aux, c)
        for s in steps:
            share = share + swap(share, "aux", s)
        theirs = swap(share, "aux", step)
        amp, *outs = gradient_share(share, theirs, denominators, jb_hi, jb_lo, range(rows), chunks[c], height, outs[0])
        amp_parts.append(amp)

    odd, even = outs[1], outs[0]
    summed = even + swap(odd, "row", 1)
    grad_ia = summed[0]
    for k in chip_order(rows):
        grad_ia = grad_ia + swap(summed[k], "row", 2 * k)
    grad_jb = gradient_jb(amp_parts, ia_parts)
    return (grad_jb, grad_ia)


def solution(mesh):
    return jax.shard_map(
        per_device,
        mesh=mesh,
        in_specs=(P("row", "aux"), P("row", "aux"), P(None, "row")),
        out_specs=(P("row", "aux"), P("row", "aux")),
        check_vma=False,
    )
```

```python
import jax
import jax.numpy as jnp
from jax import lax
from jax.experimental import pallas as pl
from jax.experimental.pallas import tpu as pltpu
from jax.sharding import PartitionSpec as P


F32, BF16 = jnp.float32, jnp.bfloat16
VMEM = pl.BlockSpec(memory_space=pltpu.VMEM)
HBM = pl.BlockSpec(memory_space=pltpu.HBM)
MIB = 1 << 20


def swap(x, axis, distance):
    size = lax.axis_size(axis)
    return lax.ppermute(x, axis, [(i, i ^ distance) for i in range(size)])


def split(x):
    hi = x.astype(BF16)
    return hi, (x - hi.astype(F32)).astype(BF16)


def mxu(a, b, dims):
    return lax.dot_general(a, b, (dims, ((), ())), preferred_element_type=F32)


def width_of(size, most):
    fits = [w for w in range(128, min(size, most) + 1, 128) if size % w == 0]
    return fits[-1] if fits else size


def prepare(factor_jb):
    height, width = factor_jb.shape
    piece = width_of(height, 128)
    pieces = height // piece
    step = width_of(width, 1024)

    def kernel(jb, hi, lo, hi_t, lo_t, held, sems):
        def copy(p):
            at = pl.ds(p * piece, piece)
            return pltpu.make_async_copy(jb.at[at], held.at[at], sems.at[p])

        for p in range(pieces):
            copy(p).start()
        for p in range(pieces):
            copy(p).wait()
            rows = pl.ds(p * piece, piece)

            @pl.loop(0, width // step)
            def _(c, rows=rows):
                columns = pl.ds(pl.multiple_of(c * step, step), step)
                a, b = split(held[rows, columns])
                hi[rows, columns], lo[rows, columns] = a, b
                hi_t[columns, rows], lo_t[columns, rows] = a.T, b.T

    plain = jax.ShapeDtypeStruct((height, width), BF16)
    turned = jax.ShapeDtypeStruct((width, height), BF16)
    return pl.pallas_call(
        kernel,
        name="prepare",
        out_shape=(plain, plain, turned, turned),
        in_specs=[HBM],
        out_specs=(VMEM,) * 4,
        scratch_shapes=[pltpu.VMEM((height, width), F32), pltpu.SemaphoreType.DMA((pieces,))],
        compiler_params=pltpu.CompilerParams(vmem_limit_bytes=38 * MIB),
        cost_estimate=pl.CostEstimate(flops=4 * height * width, bytes_accessed=4 * height * width, transcendentals=0),
    )(factor_jb)


def integral_share(blocks, hi_t, lo_t):
    n = len(blocks)
    height, width = blocks[0].shape
    rows = n * height
    columns = hi_t.shape[1]
    tile = width_of(columns, 128)

    def kernel(*refs):
        block_refs, (hi, lo, out, parts) = refs[:n], refs[n:]
        for pair in range(n // 2):
            x = jnp.concatenate([block_refs[2 * pair][...], block_refs[2 * pair + 1][...]])
            a, b = split(x)
            at = 2 * height * pair
            parts[pl.ds(at, 2 * height)] = a
            parts[pl.ds(rows + at, 2 * height)] = b
        for t in range(columns // tile):
            at = pl.ds(t * tile, tile)
            both = mxu(parts[...], hi[:, at], ((1,), (0,)))
            rest = mxu(parts[pl.ds(0, rows)], lo[:, at], ((1,), (0,)))
            out[:, at] = both[:rows] + (both[rows:] + rest)

    return pl.pallas_call(
        kernel,
        out_shape=(jax.ShapeDtypeStruct((rows, columns), F32), jax.ShapeDtypeStruct((2 * rows, width), BF16)),
        in_specs=[VMEM] * (n + 2),
        out_specs=(VMEM, VMEM),
        compiler_params=pltpu.CompilerParams(vmem_limit_bytes=20 * MIB),
        cost_estimate=pl.CostEstimate(flops=6 * rows * width * columns, bytes_accessed=MIB, transcendentals=0),
    )(*blocks, hi_t, lo_t)


def gradient_share(mine, theirs, denominators, jb_hi, jb_lo, distances, height):
    rows, columns = mine.shape
    width = jb_hi.shape[1]
    n = len(distances)
    tile = width_of(width, 512)

    def kernel(mine, theirs, denom, hi, lo, parts, *rest):
        outs, amp = rest[:n], rest[n]
        me = lax.axis_index("row")
        for slot, d in enumerate(distances):
            at = pl.multiple_of((me ^ d) * height, height)
            here = pl.ds(slot * height, height)
            amp[here] = (mine[here] + theirs[here]) / denom[pl.ds(at, height)]
        a, b = split(amp[...])
        parts[pl.ds(0, rows)] = a
        parts[pl.ds(rows, rows)] = b
        for t in range(width // tile):
            at = pl.ds(t * tile, tile)
            both = mxu(parts[...], hi[:, at], ((1,), (0,)))
            rest = mxu(parts[pl.ds(0, rows)], lo[:, at], ((1,), (0,)))
            total = both[:rows] + (both[rows:] + rest)
            for slot in range(n):
                outs[slot][:, at] = total[slot * height : (slot + 1) * height]

    block = jax.ShapeDtypeStruct((height, width), F32)
    amp, *outs = pl.pallas_call(
        kernel,
        out_shape=(jax.ShapeDtypeStruct((2 * rows, columns), BF16),) + (block,) * n,
        in_specs=[VMEM] * 5,
        out_specs=(VMEM,) * (1 + n),
        scratch_shapes=[pltpu.VMEM((rows, columns), F32)],
        compiler_params=pltpu.CompilerParams(vmem_limit_bytes=20 * MIB),
        cost_estimate=pl.CostEstimate(flops=6 * rows * width * columns, bytes_accessed=MIB, transcendentals=0),
    )(mine, theirs, denominators, jb_hi, jb_lo)
    return amp, dict(zip(distances, outs))


def gradient_jb(amp_parts, ia_parts):
    n = len(amp_parts)
    width, columns = ia_parts[0].shape[1], amp_parts[0].shape[1]
    deep = 3 * sum(i.shape[0] for i in ia_parts) // 2
    tile = width_of(width, 512)
    tiles = width // tile

    def kernel(*refs):
        amps, ias, (out, left, held, sems) = refs[:n], refs[n : 2 * n], refs[2 * n :]
        pieces = []
        for amp in amps:
            rows = amp.shape[0] // 2
            hi, lo = amp[pl.ds(0, rows)].astype(F32), amp[pl.ds(rows, rows)].astype(F32)
            pieces += [hi, lo, hi]
        left[...] = jnp.concatenate(pieces).T.astype(BF16)
        copies = []
        for t in range(tiles):
            here = pl.ds(t * tile, tile)
            pieces = []
            for ia in ias:
                rows = ia.shape[0] // 2
                hi, lo = ia[pl.ds(0, rows), here], ia[pl.ds(rows, rows), here]
                pieces += [hi, hi, lo]
            held[t] = mxu(left[...], jnp.concatenate(pieces), ((1,), (0,)))
            copies.append(pltpu.make_async_copy(held.at[t], out.at[:, here], sems.at[t]))
            copies[-1].start()
        for copy in copies:
            copy.wait()

    return pl.pallas_call(
        kernel,
        name="gradient_jb",
        out_shape=jax.ShapeDtypeStruct((columns, width), F32),
        in_specs=[VMEM] * (2 * n),
        out_specs=HBM,
        scratch_shapes=[
            pltpu.VMEM((columns, deep), BF16),
            pltpu.VMEM((tiles, columns, tile), F32),
            pltpu.SemaphoreType.DMA((tiles,)),
        ],
        compiler_params=pltpu.CompilerParams(vmem_limit_bytes=20 * MIB),
        cost_estimate=pl.CostEstimate(
            flops=2 * deep * width * columns, bytes_accessed=4 * width * columns, transcendentals=0
        ),
    )(*amp_parts, *ia_parts)


def chunks_of(rows):
    chips = range(1, rows // 2)
    last = [k for k in chips if k % 4 == 3]
    return [[*sorted(set(chips) - set(last), reverse=True), 0], last]


def aux_steps(aux):
    return aux.bit_length() - 1


def exchange(x, step):
    rows, aux = lax.axis_size("row"), lax.axis_size("aux")
    steps = aux_steps(aux)

    def partner(row, column):
        bit = (step + row % 2 * (steps // 2)) % steps
        return row * aux + (column ^ 1 << bit)

    pairs = [(row * aux + column, partner(row, column)) for row in range(rows) for column in range(aux)]
    return lax.ppermute(x, ("row", "aux"), pairs)


def per_device(factor_ia, factor_jb, denominators):
    rows = lax.axis_size("row")
    aux = lax.axis_size("aux")
    height = factor_ia.shape[0]

    blocks = {0: factor_ia}
    for k in range(1, rows // 2):
        blocks[2 * k] = swap(factor_ia, "row", 2 * k)
    for d in range(0, rows, 2):
        blocks[d + 1] = swap(blocks[d], "row", 1)
    jb_hi, jb_lo, hi_t, lo_t = prepare(factor_jb)

    amp_parts, ia_parts, sums = [], [], []
    for ks in chunks_of(rows):
        distances = [d for k in ks for d in (2 * k, 2 * k + 1)]
        share, ia = integral_share([blocks[d] for d in distances], hi_t, lo_t)
        for step in range(aux_steps(aux) - 1):
            share = share + exchange(share, step)
        theirs = exchange(share, aux_steps(aux) - 1)
        amp, outs = gradient_share(share, theirs, denominators, jb_hi, jb_lo, distances, height)
        for k in ks:
            folded = outs[2 * k] + swap(outs[2 * k + 1], "row", 1)
            sums.append(swap(folded, "row", 2 * k) if k else folded)
        amp_parts.append(amp)
        ia_parts.append(ia)

    grad_ia = sums[0]
    for part in sums[1:]:
        grad_ia = grad_ia + part
    grad_jb = gradient_jb(amp_parts, ia_parts)
    return (grad_jb, grad_ia)


def solution(mesh):
    return jax.shard_map(
        per_device,
        mesh=mesh,
        in_specs=(P("row", "aux"), P("row", "aux"), P(None, "row")),
        out_specs=(P("row", "aux"), P("row", "aux")),
        check_vma=False,
    )
```

```python
import jax
import jax.numpy as jnp
from jax import lax
from jax.experimental import pallas as pl
from jax.experimental.pallas import tpu as pltpu
from jax.sharding import PartitionSpec as P


F32, BF16 = jnp.float32, jnp.bfloat16
VMEM = pl.BlockSpec(memory_space=pltpu.VMEM)
HBM = pl.BlockSpec(memory_space=pltpu.HBM)
MIB = 1 << 20


def swap(x, axis, distance):
    size = lax.axis_size(axis)
    return lax.ppermute(x, axis, [(i, i ^ distance) for i in range(size)])


def split(x):
    hi = x.astype(BF16)
    return hi, (x - hi.astype(F32)).astype(BF16)


def mxu(a, b, dims):
    return lax.dot_general(a, b, (dims, ((), ())), preferred_element_type=F32)


def width_of(size, most):
    fits = [w for w in range(128, min(size, most) + 1, 128) if size % w == 0]
    return fits[-1] if fits else size


def prepare(factor_jb):
    height, width = factor_jb.shape
    piece = width_of(height, 128)
    pieces = height // piece
    step = width_of(width, 1024)

    def kernel(jb, hi, lo, hi_t, lo_t, held, sems):
        def copy(p):
            at = pl.ds(p * piece, piece)
            return pltpu.make_async_copy(jb.at[at], held.at[at], sems.at[p])

        for p in range(pieces):
            copy(p).start()
        for p in range(pieces):
            copy(p).wait()
            rows = pl.ds(p * piece, piece)

            for c in range(width // step):
                columns = pl.ds(c * step, step)
                a, b = split(held[rows, columns])
                hi[rows, columns], lo[rows, columns] = a, b
                hi_t[columns, rows], lo_t[columns, rows] = a.T, b.T

    plain = jax.ShapeDtypeStruct((height, width), BF16)
    turned = jax.ShapeDtypeStruct((width, height), BF16)
    return pl.pallas_call(
        kernel,
        name="prepare",
        out_shape=(plain, plain, turned, turned),
        in_specs=[HBM],
        out_specs=(VMEM,) * 4,
        scratch_shapes=[pltpu.VMEM((height, width), F32), pltpu.SemaphoreType.DMA((pieces,))],
        compiler_params=pltpu.CompilerParams(vmem_limit_bytes=38 * MIB),
        cost_estimate=pl.CostEstimate(flops=4 * height * width, bytes_accessed=4 * height * width, transcendentals=0),
    )(factor_jb)


def integral_share(blocks, hi_t, lo_t):
    n = len(blocks)
    height, width = blocks[0].shape
    rows = n * height
    columns = hi_t.shape[1]
    tile = width_of(columns, 128)

    def kernel(*refs):
        block_refs, (hi, lo, out, parts) = refs[:n], refs[n:]
        for pair in range(n // 2):
            x = jnp.concatenate([block_refs[2 * pair][...], block_refs[2 * pair + 1][...]])
            a, b = split(x)
            at = 2 * height * pair
            parts[pl.ds(at, 2 * height)] = a
            parts[pl.ds(rows + at, 2 * height)] = b
        for t in range(columns // tile):
            at = pl.ds(t * tile, tile)
            both = mxu(parts[...], hi[:, at], ((1,), (0,)))
            rest = mxu(parts[pl.ds(0, rows)], lo[:, at], ((1,), (0,)))
            out[:, at] = both[:rows] + (both[rows:] + rest)

    return pl.pallas_call(
        kernel,
        out_shape=(jax.ShapeDtypeStruct((rows, columns), F32), jax.ShapeDtypeStruct((2 * rows, width), BF16)),
        in_specs=[VMEM] * (n + 2),
        out_specs=(VMEM, VMEM),
        compiler_params=pltpu.CompilerParams(vmem_limit_bytes=20 * MIB),
        cost_estimate=pl.CostEstimate(flops=6 * rows * width * columns, bytes_accessed=MIB, transcendentals=0),
    )(*blocks, hi_t, lo_t)


def gradient_share(mine, theirs, denominators, jb_hi, jb_lo, distances, height):
    rows, columns = mine.shape
    width = jb_hi.shape[1]
    n = len(distances)
    tile = width_of(width, 512)

    def kernel(mine, theirs, denom, hi, lo, parts, *rest):
        outs, amp = rest[:n], rest[n]
        me = lax.axis_index("row")
        for slot, d in enumerate(distances):
            at = pl.multiple_of((me ^ d) * height, height)
            here = pl.ds(slot * height, height)
            amp[here] = (mine[here] + theirs[here]) / denom[pl.ds(at, height)]
        a, b = split(amp[...])
        parts[pl.ds(0, rows)] = a
        parts[pl.ds(rows, rows)] = b
        for t in range(width // tile):
            at = pl.ds(t * tile, tile)
            both = mxu(parts[...], hi[:, at], ((1,), (0,)))
            rest = mxu(parts[pl.ds(0, rows)], lo[:, at], ((1,), (0,)))
            total = both[:rows] + (both[rows:] + rest)
            for slot in range(n):
                outs[slot][:, at] = total[slot * height : (slot + 1) * height]

    block = jax.ShapeDtypeStruct((height, width), F32)
    amp, *outs = pl.pallas_call(
        kernel,
        out_shape=(jax.ShapeDtypeStruct((2 * rows, columns), BF16),) + (block,) * n,
        in_specs=[VMEM] * 5,
        out_specs=(VMEM,) * (1 + n),
        scratch_shapes=[pltpu.VMEM((rows, columns), F32)],
        compiler_params=pltpu.CompilerParams(vmem_limit_bytes=20 * MIB),
        cost_estimate=pl.CostEstimate(flops=6 * rows * width * columns, bytes_accessed=MIB, transcendentals=0),
    )(mine, theirs, denominators, jb_hi, jb_lo)
    return amp, dict(zip(distances, outs))


def gradient_jb(amp_parts, ia_parts):
    n = len(amp_parts)
    width, columns = ia_parts[0].shape[1], amp_parts[0].shape[1]
    deep = 3 * sum(i.shape[0] for i in ia_parts) // 2
    tile = width_of(width, 512)
    tiles = width // tile

    def kernel(*refs):
        amps, ias, (out, left, held, sems) = refs[:n], refs[n : 2 * n], refs[2 * n :]
        pieces = []
        for amp in amps:
            rows = amp.shape[0] // 2
            hi, lo = amp[pl.ds(0, rows)].astype(F32), amp[pl.ds(rows, rows)].astype(F32)
            pieces += [hi, lo, hi]
        left[...] = jnp.concatenate(pieces).T.astype(BF16)
        copies = []
        for t in range(tiles):
            here = pl.ds(t * tile, tile)
            pieces = []
            for ia in ias:
                rows = ia.shape[0] // 2
                hi, lo = ia[pl.ds(0, rows), here], ia[pl.ds(rows, rows), here]
                pieces += [hi, hi, lo]
            held[t] = mxu(left[...], jnp.concatenate(pieces), ((1,), (0,)))
            copies.append(pltpu.make_async_copy(held.at[t], out.at[:, here], sems.at[t]))
            copies[-1].start()
        for copy in copies:
            copy.wait()

    return pl.pallas_call(
        kernel,
        name="gradient_jb",
        out_shape=jax.ShapeDtypeStruct((columns, width), F32),
        in_specs=[VMEM] * (2 * n),
        out_specs=HBM,
        scratch_shapes=[
            pltpu.VMEM((columns, deep), BF16),
            pltpu.VMEM((tiles, columns, tile), F32),
            pltpu.SemaphoreType.DMA((tiles,)),
        ],
        compiler_params=pltpu.CompilerParams(vmem_limit_bytes=20 * MIB),
        cost_estimate=pl.CostEstimate(
            flops=2 * deep * width * columns, bytes_accessed=4 * width * columns, transcendentals=0
        ),
    )(*amp_parts, *ia_parts)


def chunks_of(rows):
    chips = range(1, rows // 2)
    last = [k for k in chips if k % 2 and k > 1]
    return [[*sorted(set(chips) - set(last), reverse=True), 0], last]


def aux_steps(aux):
    return aux.bit_length() - 1


def exchange(x, step):
    rows, aux = lax.axis_size("row"), lax.axis_size("aux")
    steps = aux_steps(aux)

    def partner(row, column):
        bit = (step + row % 2 * (steps // 2)) % steps
        return row * aux + (column ^ 1 << bit)

    pairs = [(row * aux + column, partner(row, column)) for row in range(rows) for column in range(aux)]
    return lax.ppermute(x, ("row", "aux"), pairs)


def per_device(factor_ia, factor_jb, denominators):
    rows = lax.axis_size("row")
    aux = lax.axis_size("aux")
    height = factor_ia.shape[0]

    blocks = {0: factor_ia}
    for k in range(1, rows // 2):
        if k % 2 and k > 1:
            blocks[2 * k] = swap(blocks[2 * k - 2], "row", 2)
        else:
            blocks[2 * k] = swap(factor_ia, "row", 2 * k)
    for d in range(0, rows, 2):
        blocks[d + 1] = swap(blocks[d], "row", 1)
    jb_hi, jb_lo, hi_t, lo_t = prepare(factor_jb)

    amp_parts, ia_parts, sums = [], [], []
    for ks in chunks_of(rows):
        distances = [d for k in ks for d in (2 * k, 2 * k + 1)]
        share, ia = integral_share([blocks[d] for d in distances], hi_t, lo_t)
        for step in range(aux_steps(aux) - 1):
            share = share + exchange(share, step)
        theirs = exchange(share, aux_steps(aux) - 1)
        amp, outs = gradient_share(share, theirs, denominators, jb_hi, jb_lo, distances, height)
        for k in ks:
            folded = outs[2 * k] + swap(outs[2 * k + 1], "row", 1)
            sums.append(swap(folded, "row", 2 * k) if k else folded)
        amp_parts.append(amp)
        ia_parts.append(ia)

    grad_ia = sums[0]
    for part in sums[1:]:
        grad_ia = grad_ia + part
    grad_jb = gradient_jb(amp_parts, ia_parts)
    return (grad_jb, grad_ia)


def solution(mesh):
    return jax.shard_map(
        per_device,
        mesh=mesh,
        in_specs=(P("row", "aux"), P("row", "aux"), P(None, "row")),
        out_specs=(P("row", "aux"), P("row", "aux")),
        check_vma=False,
    )
```

```python
import jax
import jax.numpy as jnp
from jax import lax
from jax.experimental import pallas as pl
from jax.experimental.pallas import tpu as pltpu
from jax.sharding import PartitionSpec as P


F32, BF16 = jnp.float32, jnp.bfloat16
VMEM = pl.BlockSpec(memory_space=pltpu.VMEM)
HBM = pl.BlockSpec(memory_space=pltpu.HBM)
MIB = 1 << 20


def swap(x, axis, distance):
    size = lax.axis_size(axis)
    return lax.ppermute(x, axis, [(i, i ^ distance) for i in range(size)])


def split(x):
    hi = x.astype(BF16)
    return hi, (x - hi.astype(F32)).astype(BF16)


def mxu(a, b, dims):
    return lax.dot_general(a, b, (dims, ((), ())), preferred_element_type=F32)


def width_of(size, most):
    fits = [w for w in range(128, min(size, most) + 1, 128) if size % w == 0]
    return fits[-1] if fits else size


def prepare(factor_jb):
    height, width = factor_jb.shape
    piece = width_of(height, 128)
    pieces = height // piece
    step = width_of(width, 1024)

    def kernel(jb, hi, lo, hi_t, lo_t, held, sems):
        def copy(p):
            at = pl.ds(p * piece, piece)
            return pltpu.make_async_copy(jb.at[at], held.at[at], sems.at[p])

        for p in range(pieces):
            copy(p).start()
        for p in range(pieces):
            copy(p).wait()
            rows = pl.ds(p * piece, piece)

            for c in range(width // step):
                columns = pl.ds(c * step, step)
                a, b = split(held[rows, columns])
                hi[rows, columns], lo[rows, columns] = a, b
                hi_t[columns, rows], lo_t[columns, rows] = a.T, b.T

    plain = jax.ShapeDtypeStruct((height, width), BF16)
    turned = jax.ShapeDtypeStruct((width, height), BF16)
    return pl.pallas_call(
        kernel,
        name="prepare",
        out_shape=(plain, plain, turned, turned),
        in_specs=[HBM],
        out_specs=(VMEM,) * 4,
        scratch_shapes=[pltpu.VMEM((height, width), F32), pltpu.SemaphoreType.DMA((pieces,))],
        compiler_params=pltpu.CompilerParams(vmem_limit_bytes=38 * MIB),
        cost_estimate=pl.CostEstimate(flops=4 * height * width, bytes_accessed=4 * height * width, transcendentals=0),
    )(factor_jb)


def integral_share(blocks, hi_t, lo_t):
    n = len(blocks)
    height, width = blocks[0].shape
    rows = n * height
    columns = hi_t.shape[1]
    tile = width_of(columns, 128)

    def kernel(*refs):
        block_refs, (hi, lo, out, parts) = refs[:n], refs[n:]
        for pair in range(n // 2):
            x = jnp.concatenate([block_refs[2 * pair][...], block_refs[2 * pair + 1][...]])
            a, b = split(x)
            at = 2 * height * pair
            parts[pl.ds(at, 2 * height)] = a
            parts[pl.ds(rows + at, 2 * height)] = b
        for t in range(columns // tile):
            at = pl.ds(t * tile, tile)
            both = mxu(parts[...], hi[:, at], ((1,), (0,)))
            rest = mxu(parts[pl.ds(0, rows)], lo[:, at], ((1,), (0,)))
            out[:, at] = both[:rows] + (both[rows:] + rest)

    return pl.pallas_call(
        kernel,
        out_shape=(jax.ShapeDtypeStruct((rows, columns), F32), jax.ShapeDtypeStruct((2 * rows, width), BF16)),
        in_specs=[VMEM] * (n + 2),
        out_specs=(VMEM, VMEM),
        compiler_params=pltpu.CompilerParams(vmem_limit_bytes=20 * MIB),
        cost_estimate=pl.CostEstimate(flops=6 * rows * width * columns, bytes_accessed=MIB, transcendentals=0),
    )(*blocks, hi_t, lo_t)


def gradient_share(mine, theirs, denominators, jb_hi, jb_lo, distances, height):
    rows, columns = mine.shape
    width = jb_hi.shape[1]
    n = len(distances)
    tile = width_of(width, 512)

    def kernel(mine, theirs, denom, hi, lo, parts, *rest):
        outs, amp = rest[:n], rest[n]
        me = lax.axis_index("row")
        for slot, d in enumerate(distances):
            at = pl.multiple_of((me ^ d) * height, height)
            here = pl.ds(slot * height, height)
            amp[here] = (mine[here] + theirs[here]) / denom[pl.ds(at, height)]
        a, b = split(amp[...])
        parts[pl.ds(0, rows)] = a
        parts[pl.ds(rows, rows)] = b
        for t in range(width // tile):
            at = pl.ds(t * tile, tile)
            both = mxu(parts[...], hi[:, at], ((1,), (0,)))
            rest = mxu(parts[pl.ds(0, rows)], lo[:, at], ((1,), (0,)))
            total = both[:rows] + (both[rows:] + rest)
            for slot in range(n):
                outs[slot][:, at] = total[slot * height : (slot + 1) * height]

    block = jax.ShapeDtypeStruct((height, width), F32)
    amp, *outs = pl.pallas_call(
        kernel,
        out_shape=(jax.ShapeDtypeStruct((2 * rows, columns), BF16),) + (block,) * n,
        in_specs=[VMEM] * 5,
        out_specs=(VMEM,) * (1 + n),
        scratch_shapes=[pltpu.VMEM((rows, columns), F32)],
        compiler_params=pltpu.CompilerParams(vmem_limit_bytes=20 * MIB),
        cost_estimate=pl.CostEstimate(flops=6 * rows * width * columns, bytes_accessed=MIB, transcendentals=0),
    )(mine, theirs, denominators, jb_hi, jb_lo)
    return amp, dict(zip(distances, outs))


def gradient_jb(amp_parts, ia_parts):
    n = len(amp_parts)
    width, columns = ia_parts[0].shape[1], amp_parts[0].shape[1]
    deep = 3 * sum(i.shape[0] for i in ia_parts) // 2
    tile = width_of(width, 512)
    tiles = width // tile

    def kernel(*refs):
        amps, ias, (out, left, held, sems) = refs[:n], refs[n : 2 * n], refs[2 * n :]
        pieces = []
        for amp in amps:
            rows = amp.shape[0] // 2
            hi, lo = amp[pl.ds(0, rows)].astype(F32), amp[pl.ds(rows, rows)].astype(F32)
            pieces += [hi, lo, hi]
        left[...] = jnp.concatenate(pieces).T.astype(BF16)
        copies = []
        for t in range(tiles):
            here = pl.ds(t * tile, tile)
            pieces = []
            for ia in ias:
                rows = ia.shape[0] // 2
                hi, lo = ia[pl.ds(0, rows), here], ia[pl.ds(rows, rows), here]
                pieces += [hi, hi, lo]
            held[t] = mxu(left[...], jnp.concatenate(pieces), ((1,), (0,)))
            copies.append(pltpu.make_async_copy(held.at[t], out.at[:, here], sems.at[t]))
            copies[-1].start()
        for copy in copies:
            copy.wait()

    return pl.pallas_call(
        kernel,
        name="gradient_jb",
        out_shape=jax.ShapeDtypeStruct((columns, width), F32),
        in_specs=[VMEM] * (2 * n),
        out_specs=HBM,
        scratch_shapes=[
            pltpu.VMEM((columns, deep), BF16),
            pltpu.VMEM((tiles, columns, tile), F32),
            pltpu.SemaphoreType.DMA((tiles,)),
        ],
        compiler_params=pltpu.CompilerParams(vmem_limit_bytes=20 * MIB),
        cost_estimate=pl.CostEstimate(
            flops=2 * deep * width * columns, bytes_accessed=4 * width * columns, transcendentals=0
        ),
    )(*amp_parts, *ia_parts)


def chunks_of(rows):
    chips = range(1, rows // 2)
    last = [k for k in chips if k % 2 and k > 1]
    return [[*sorted(set(chips) - set(last), reverse=True), 0], last]


def aux_steps(aux):
    return aux.bit_length() - 1


def exchange(x, step):
    rows, aux = lax.axis_size("row"), lax.axis_size("aux")
    steps = aux_steps(aux)

    def partner(row, column):
        if straight(aux):
            return row * aux + (column ^ ((1, 2, 3), (2, 1, 3))[row % 2][step])
        bit = (step + row % 2 * (steps // 2)) % steps
        return row * aux + (column ^ 1 << bit)

    pairs = [(row * aux + column, partner(row, column)) for row in range(rows) for column in range(aux)]
    return lax.ppermute(x, ("row", "aux"), pairs)


def straight(aux):
    return aux == 4


def aux_sum(share):
    aux = lax.axis_size("aux")
    steps = aux_steps(aux)
    if straight(aux):
        one, two, three = (exchange(share, step) for step in range(3))
        return share + one, two + three
    for step in range(steps - 1):
        share = share + exchange(share, step)
    return share, exchange(share, steps - 1)


def per_device(factor_ia, factor_jb, denominators):
    rows = lax.axis_size("row")
    height = factor_ia.shape[0]

    blocks = {0: factor_ia}
    for k in range(1, rows // 2):
        if k % 2 and k > 1:
            blocks[2 * k] = swap(blocks[2 * k - 2], "row", 2)
        else:
            blocks[2 * k] = swap(factor_ia, "row", 2 * k)
    for d in range(0, rows, 2):
        blocks[d + 1] = swap(blocks[d], "row", 1)
    jb_hi, jb_lo, hi_t, lo_t = prepare(factor_jb)

    amp_parts, ia_parts, sums = [], [], []
    for ks in chunks_of(rows):
        distances = [d for k in ks for d in (2 * k, 2 * k + 1)]
        share, ia = integral_share([blocks[d] for d in distances], hi_t, lo_t)
        mine, theirs = aux_sum(share)
        amp, outs = gradient_share(mine, theirs, denominators, jb_hi, jb_lo, distances, height)
        for k in ks:
            theirs = swap(outs[2 * k + 1], "row", 1)
            folded = outs[2 * k] + theirs
            sums.append(swap(folded, "row", 2 * k) if k else folded)
        amp_parts.append(amp)
        ia_parts.append(ia)

    grad_ia = sums[0]
    for part in sums[1:]:
        grad_ia = grad_ia + part
    grad_jb = gradient_jb(amp_parts, ia_parts)
    return (grad_jb, grad_ia)


def solution(mesh):
    return jax.shard_map(
        per_device,
        mesh=mesh,
        in_specs=(P("row", "aux"), P("row", "aux"), P(None, "row")),
        out_specs=(P("row", "aux"), P("row", "aux")),
        check_vma=False,
    )
```

```python
import jax
import jax.numpy as jnp
from jax import lax
from jax.experimental import pallas as pl
from jax.experimental.pallas import tpu as pltpu
from jax.sharding import PartitionSpec as P


F32, BF16 = jnp.float32, jnp.bfloat16
VMEM = pl.BlockSpec(memory_space=pltpu.VMEM)
HBM = pl.BlockSpec(memory_space=pltpu.HBM)
MIB = 1 << 20


def swap(x, axis, distance):
    size = lax.axis_size(axis)
    return lax.ppermute(x, axis, [(i, i ^ distance) for i in range(size)])


def split(x):
    hi = x.astype(BF16)
    return hi, (x - hi.astype(F32)).astype(BF16)


def mxu(a, b, dims):
    return lax.dot_general(a, b, (dims, ((), ())), preferred_element_type=F32)


def width_of(size, most):
    fits = [w for w in range(128, min(size, most) + 1, 128) if size % w == 0]
    return fits[-1] if fits else size


def prepare(factor_jb):
    height, width = factor_jb.shape
    piece = width_of(height, 128)
    pieces = height // piece
    step = width_of(width, 256)

    def kernel(jb, hi, lo, hi_t, lo_t, held, sems):
        def copy(p):
            at = pl.ds(p * piece, piece)
            return pltpu.make_async_copy(jb.at[at], held.at[at], sems.at[p])

        for p in range(pieces):
            copy(p).start()
        for p in range(pieces):
            copy(p).wait()
            rows = pl.ds(p * piece, piece)

            for c in range(width // step):
                columns = pl.ds(c * step, step)
                a, b = split(held[rows, columns])
                hi[rows, columns], lo[rows, columns] = a, b
                hi_t[columns, rows], lo_t[columns, rows] = a.T, b.T

    plain = jax.ShapeDtypeStruct((height, width), BF16)
    turned = jax.ShapeDtypeStruct((width, height), BF16)
    return pl.pallas_call(
        kernel,
        name="prepare",
        out_shape=(plain, plain, turned, turned),
        in_specs=[HBM],
        out_specs=(VMEM,) * 4,
        scratch_shapes=[pltpu.VMEM((height, width), F32), pltpu.SemaphoreType.DMA((pieces,))],
        compiler_params=pltpu.CompilerParams(vmem_limit_bytes=38 * MIB),
        cost_estimate=pl.CostEstimate(flops=4 * height * width, bytes_accessed=4 * height * width, transcendentals=0),
    )(factor_jb)


def integral_share(blocks, hi_t, lo_t):
    n = len(blocks)
    height, width = blocks[0].shape
    rows = n * height
    columns = hi_t.shape[1]
    tile = width_of(columns, 640)

    def kernel(*refs):
        block_refs, (hi, lo, out, parts) = refs[:n], refs[n:]
        for pair in range(n // 2):
            x = jnp.concatenate([block_refs[2 * pair][...], block_refs[2 * pair + 1][...]])
            a, b = split(x)
            at = 2 * height * pair
            parts[pl.ds(at, 2 * height)] = a
            parts[pl.ds(rows + at, 2 * height)] = b
        for t in range(columns // tile):
            at = pl.ds(t * tile, tile)
            both = mxu(parts[...], hi[:, at], ((1,), (0,)))
            rest = mxu(parts[pl.ds(0, rows)], lo[:, at], ((1,), (0,)))
            out[:, at] = both[:rows] + (both[rows:] + rest)

    return pl.pallas_call(
        kernel,
        out_shape=(jax.ShapeDtypeStruct((rows, columns), F32), jax.ShapeDtypeStruct((2 * rows, width), BF16)),
        in_specs=[VMEM] * (n + 2),
        out_specs=(VMEM, VMEM),
        compiler_params=pltpu.CompilerParams(vmem_limit_bytes=20 * MIB),
        cost_estimate=pl.CostEstimate(flops=6 * rows * width * columns, bytes_accessed=MIB, transcendentals=0),
    )(*blocks, hi_t, lo_t)


def gradient_share(mine, theirs, denominators, jb_hi, jb_lo, distances, height):
    rows, columns = mine.shape
    width = jb_hi.shape[1]
    n = len(distances)
    tile = width_of(width, 512)

    def kernel(mine, theirs, denom, hi, lo, parts, *rest):
        outs, amp = rest[:n], rest[n]
        me = lax.axis_index("row")
        for slot, d in enumerate(distances):
            at = pl.multiple_of((me ^ d) * height, height)
            here = pl.ds(slot * height, height)
            amp[here] = (mine[here] + theirs[here]) / denom[pl.ds(at, height)]
        a, b = split(amp[...])
        parts[pl.ds(0, rows)] = a
        parts[pl.ds(rows, rows)] = b
        for t in range(width // tile):
            at = pl.ds(t * tile, tile)
            both = mxu(parts[...], hi[:, at], ((1,), (0,)))
            rest = mxu(parts[pl.ds(0, rows)], lo[:, at], ((1,), (0,)))
            total = both[:rows] + (both[rows:] + rest)
            for slot in range(n):
                outs[slot][:, at] = total[slot * height : (slot + 1) * height]

    block = jax.ShapeDtypeStruct((height, width), F32)
    amp, *outs = pl.pallas_call(
        kernel,
        out_shape=(jax.ShapeDtypeStruct((2 * rows, columns), BF16),) + (block,) * n,
        in_specs=[VMEM] * 5,
        out_specs=(VMEM,) * (1 + n),
        scratch_shapes=[pltpu.VMEM((rows, columns), F32)],
        compiler_params=pltpu.CompilerParams(vmem_limit_bytes=20 * MIB),
        cost_estimate=pl.CostEstimate(flops=6 * rows * width * columns, bytes_accessed=MIB, transcendentals=0),
    )(mine, theirs, denominators, jb_hi, jb_lo)
    return amp, dict(zip(distances, outs))


def gradient_jb(amp_parts, ia_parts):
    n = len(amp_parts)
    width, columns = ia_parts[0].shape[1], amp_parts[0].shape[1]
    deep = 3 * sum(i.shape[0] for i in ia_parts) // 2
    tile = width_of(width, 512)
    tiles = width // tile

    def kernel(*refs):
        amps, ias, (out, left, held, sems) = refs[:n], refs[n : 2 * n], refs[2 * n :]
        pieces = []
        for amp in amps:
            rows = amp.shape[0] // 2
            hi, lo = amp[pl.ds(0, rows)].astype(F32), amp[pl.ds(rows, rows)].astype(F32)
            pieces += [hi, lo, hi]
        left[...] = jnp.concatenate(pieces).T.astype(BF16)
        copies = []
        for t in range(tiles):
            here = pl.ds(t * tile, tile)
            pieces = []
            for ia in ias:
                rows = ia.shape[0] // 2
                hi, lo = ia[pl.ds(0, rows), here], ia[pl.ds(rows, rows), here]
                pieces += [hi, hi, lo]
            held[t] = mxu(left[...], jnp.concatenate(pieces), ((1,), (0,)))
            copies.append(pltpu.make_async_copy(held.at[t], out.at[:, here], sems.at[t]))
            copies[-1].start()
        for copy in copies:
            copy.wait()

    return pl.pallas_call(
        kernel,
        name="gradient_jb",
        out_shape=jax.ShapeDtypeStruct((columns, width), F32),
        in_specs=[VMEM] * (2 * n),
        out_specs=HBM,
        scratch_shapes=[
            pltpu.VMEM((columns, deep), BF16),
            pltpu.VMEM((tiles, columns, tile), F32),
            pltpu.SemaphoreType.DMA((tiles,)),
        ],
        compiler_params=pltpu.CompilerParams(vmem_limit_bytes=20 * MIB),
        cost_estimate=pl.CostEstimate(
            flops=2 * deep * width * columns, bytes_accessed=4 * width * columns, transcendentals=0
        ),
    )(*amp_parts, *ia_parts)


def chunks_of(rows):
    chips = range(1, rows // 2)
    last = [k for k in chips if k % 2 and k > 1]
    return [[*sorted(set(chips) - set(last), reverse=True), 0], last]


def aux_steps(aux):
    return aux.bit_length() - 1


def exchange(x, step):
    rows, aux = lax.axis_size("row"), lax.axis_size("aux")
    steps = aux_steps(aux)

    def partner(row, column):
        if straight(aux):
            return row * aux + (column ^ ((3, 1, 2), (3, 2, 1))[row % 2][step])
        bit = (step + row % 2 * (steps // 2)) % steps
        return row * aux + (column ^ 1 << bit)

    pairs = [(row * aux + column, partner(row, column)) for row in range(rows) for column in range(aux)]
    return lax.ppermute(x, ("row", "aux"), pairs)


def straight(aux):
    return aux == 4


def aux_sum(share):
    aux = lax.axis_size("aux")
    steps = aux_steps(aux)
    if straight(aux):
        one, two, three = (exchange(share, step) for step in range(3))
        return share + one, two + three
    for step in range(steps - 1):
        share = share + exchange(share, step)
    return share, exchange(share, steps - 1)


def per_device(factor_ia, factor_jb, denominators):
    rows = lax.axis_size("row")
    height = factor_ia.shape[0]

    blocks = {0: factor_ia}
    for k in range(1, rows // 2):
        if k % 2 and k > 1:
            blocks[2 * k] = swap(blocks[2 * k - 2], "row", 2)
        else:
            blocks[2 * k] = swap(factor_ia, "row", 2 * k)
    for d in range(0, rows, 2):
        blocks[d + 1] = swap(blocks[d], "row", 1)
    jb_hi, jb_lo, hi_t, lo_t = prepare(factor_jb)

    amp_parts, ia_parts, sums = [], [], []
    for ks in chunks_of(rows):
        distances = [d for k in ks for d in (2 * k, 2 * k + 1)]
        share, ia = integral_share([blocks[d] for d in distances], hi_t, lo_t)
        mine, theirs = aux_sum(share)
        amp, outs = gradient_share(mine, theirs, denominators, jb_hi, jb_lo, distances, height)
        for k in ks:
            theirs = swap(outs[2 * k + 1], "row", 1)
            folded = outs[2 * k] + theirs
            sums.append(swap(folded, "row", 2 * k) if k else folded)
        amp_parts.append(amp)
        ia_parts.append(ia)

    grad_ia = sums[0]
    for part in sums[1:]:
        grad_ia = grad_ia + part
    grad_jb = gradient_jb(amp_parts, ia_parts)
    return (grad_jb, grad_ia)


def solution(mesh):
    return jax.shard_map(
        per_device,
        mesh=mesh,
        in_specs=(P("row", "aux"), P("row", "aux"), P(None, "row")),
        out_specs=(P("row", "aux"), P("row", "aux")),
        check_vma=False,
    )
```
